128 devices in a mesh: gx: 8 (over x, core), gy: 8 (over y, z_lo), ga: 2 (over z_hi).
Axes of the slice: x: 4, y: 4, z: 4 (z_hi: 2, z_lo: 2; z = z_hi * 2 + z_lo), core: 2. Of those that a mesh axis runs over, the one named last changes fastest.
Arguments:
- level_set: float32 [256, 256, 512], P('gx', 'gy', 'ga'), may hold values from -2 to 2
- displacement_prev: float32 [3, 256, 256, 512], P(None, 'gx', 'gy', 'ga'), may hold values from -6 to 6
- traction: float32 [3], replicated, may hold values from -3 to 3
- load_mask: int32 [256, 256, 512], P('gx', 'gy', 'ga'), may hold values 0 or 1
- support_mask: int32 [256, 256, 512], P('gx', 'gy', 'ga'), may hold values 0 or 1
- extension: bfloat16 [256, 256], P('gy'), as said below
- tile_count: int32 [8, 16], replicated, may hold values from 1 to 8, 64 in all within a row
- tile_list: int32 [128, 8], P(('gx', 'gy', 'ga')), may hold values from 0 to 7, each once within a row
Outputs:
- displacement: float32 [3, 256, 256, 512], P(None, 'gx', 'gy', 'ga')
- level_set_new: float32 [256, 256, 512], P('gx', 'gy', 'ga')
The draws below stay inside these ranges and needn't reach their ends.
Inputs may be any that keep to these rules, and one draw needn't show every extreme that they name: Each row of tile_count sums to 64. Each row of tile_list is a permutation; only the first tile_count entries of a device's row are read. extension is symmetric.
All inputs are finite; a program needn't handle non-finite values. No bound on the sum of `load_mask` or of `support_mask` on one device may be relied on, other than what follows from the above.
Results may differ from the reference program's by a relative error of at most 0.0014.
Values may be sent and summed in bfloat16 or wider, within the bound.
No kernel may reach another device: no remote copies, remote signals or barrier semaphores. Data moves between devices by JAX's collectives and lax.ppermute only.
A program may use at most 256 MiB of HBM per device.

```python
import math
import jax
import jax.numpy as jnp
import numpy as np
from jax import lax

TILE = 32
CX = 32
CY = 32
CZ = 256
JACOBI = 3
SWEEPS = 4
TPD = 8
GROUP = 16
NX = 256
NY = 256
NZ = 512
N_GX = 8
N_GY = 8
N_GA = 2
DEVICES = 128


def draw_extension(key, part):
    raw_values = jax.random.normal(key, (NY, NY), jnp.float32)
    symmetric = 0.5 * (raw_values + raw_values.T) * (0.6 / math.sqrt(NY))
    return (symmetric + jnp.eye(NY, dtype=jnp.float32)).astype(jnp.bfloat16)


def with_ends(values, rng, low, largest):
    spot = [jax.random.randint(jax.random.fold_in(rng, axis), (), 0, length) for axis, length in enumerate(values.shape)]
    widest = values.shape.index(max(values.shape))
    beside = spot[:widest] + [(spot[widest] + 1) % values.shape[widest]] + spot[widest + 1:]
    return values.at[tuple(spot)].set(low).at[tuple(beside)].set(largest)


def shard_levels(key, extent, shards, smallest, high):
    loudness = 1.0
    for axis_at, parts in shards:
        draws = jax.random.uniform(jax.random.fold_in(jax.random.fold_in(key, 6), axis_at), (parts,), jnp.float32, smallest / len(shards), high / len(shards))
        loudness = loudness * jnp.repeat(jnp.exp(draws), extent[axis_at] // parts).reshape((-1,) + (1,) * (len(extent) - 1 - axis_at))
    return loudness


def profile(count, total, most, skew):
    portions = [(1 << 20) // math.isqrt(standing ** skew) + 1 for standing in range(2, count + 1)]
    rest, given = total - most - (count - 1), [1] * (count - 1)
    while rest > 0:
        candidates = [i for i in range(count - 1) if given[i] < most]
        whole, budget = sum([portions[i] for i in candidates]), rest
        for i in candidates:
            addition = min(most - given[i], max(1, budget * portions[i] // whole), rest)
            given[i] = given[i] + addition
            rest = rest - addition
    return np.array([most] + given)


def uneven(rng, count, total, reach, skew):
    if count == 2:
        one = jax.random.randint(rng, (), max(1, total - reach), min(reach, total - 1) + 1)
        return jnp.stack([one, total - one])
    sizes = jnp.asarray(profile(count, total, reach, skew), jnp.int32)
    couples = (count - 1) // 2
    source_of, taker = sizes[1:1 + 2 * couples:2], sizes[2:2 + 2 * couples:2]
    slack = jnp.minimum(source_of - 1, reach - taker)
    passed = jax.random.randint(jax.random.fold_in(rng, 1), (couples,), 0, 1 << 20) % (slack + 1)
    sizes = sizes.at[1:1 + 2 * couples:2].set(source_of - passed).at[2:2 + 2 * couples:2].set(taker + passed)
    return sizes[jax.random.permutation(jax.random.fold_in(rng, 2), count)]


def scatter_about(stream_key, extent, scale, most, pieces=(), kind=jnp.bfloat16):
    values = scale * jax.random.normal(stream_key, extent, jnp.float32)
    if pieces:
        values = values * shard_levels(stream_key, extent, pieces, -0.22, 0.18)
    return jnp.clip(values, -most, most).astype(kind)


def setup_inputs(seed: int = 0) -> dict:
    keys = jax.random.split(jax.random.key(seed), 9)
    return {
        "level_set": jnp.clip(jax.random.uniform(keys[0], (NX, NY, NZ), jnp.float32, -2.0, 2.0) * shard_levels(keys[0], (NX, NY, NZ), ((0, 8), (1, 8), (2, 2)), -0.4, 0.0), -2.0, 2.0),
        "displacement_prev": scatter_about(keys[1], (3, NX, NY, NZ), 1.0, 6.0, ((1, 8), (2, 8), (3, 2)), jnp.float32),
        "traction": scatter_about(keys[2], (3,), 1.0, 3.0, (), jnp.float32),
        "load_mask": with_ends((jax.random.randint(keys[3], (NX, NY, NZ), 0, 4) < 1).astype(jnp.int32), jax.random.fold_in(keys[3], 1), 0, 1),
        "support_mask": with_ends((jax.random.randint(keys[4], (NX, NY, NZ), 0, 8) < 1).astype(jnp.int32), jax.random.fold_in(keys[4], 1), 0, 1),
        "extension": draw_extension(jax.random.fold_in(keys[8], 71), 0),
        "tile_count": jax.vmap(lambda own: uneven(own, GROUP, TPD * GROUP // 2, TPD, 2))(jax.random.split(keys[6], N_GX)).reshape((N_GX, GROUP)).astype(jnp.int32),
        "tile_list": jax.vmap(lambda own: jax.random.permutation(own, TPD))(jax.random.split(keys[7], DEVICES)).reshape((DEVICES, TPD)).astype(jnp.int32),
    }


emin = 0.05
coupling = 0.5
relax = 0.6
advance_step = 0.5
pseudo_step = 0.3

def stiffness(level_values):
    return emin + (1.0 - emin) * 0.5 * (1.0 + jnp.tanh(level_values))

def face_weights(padded_e):
    centre = padded_e[1:-1, 1:-1, 1:-1]
    beside = [padded_e[:-2, 1:-1, 1:-1], padded_e[2:, 1:-1, 1:-1], padded_e[1:-1, :-2, 1:-1], padded_e[1:-1, 2:, 1:-1], padded_e[1:-1, 1:-1, :-2], padded_e[1:-1, 1:-1, 2:]]
    return [0.5 * (centre + neighbour) for neighbour in beside]

def operate(padded_u, weights, centre_e):
    inner = padded_u[:, 1:-1, 1:-1, 1:-1]
    beside = [padded_u[:, :-2, 1:-1, 1:-1], padded_u[:, 2:, 1:-1, 1:-1], padded_u[:, 1:-1, :-2, 1:-1], padded_u[:, 1:-1, 2:, 1:-1], padded_u[:, 1:-1, 1:-1, :-2], padded_u[:, 1:-1, 1:-1, 2:]]
    result = coupling * centre_e[None] * lax.optimization_barrier(jnp.sum(inner, axis=0, keepdims=True))
    for weight, neighbour in zip(weights, beside):
        result = result + weight[None] * (inner - neighbour)
    return result

def godunov(values, earlier, further):
    growing = jnp.zeros_like(values)
    shrinking = jnp.zeros_like(values)
    for below, above in zip(earlier, further):
        behind_step = values - below
        ahead_step = above - values
        growing = growing + jnp.maximum(jnp.square(jnp.maximum(behind_step, 0.0)), jnp.square(jnp.minimum(ahead_step, 0.0)))
        shrinking = shrinking + jnp.maximum(jnp.square(jnp.minimum(behind_step, 0.0)), jnp.square(jnp.maximum(ahead_step, 0.0)))
    return (growing, shrinking)

def reinit_tiles(start_values):
    sign_field = start_values / jnp.sqrt(start_values * start_values + 1.0)
    values = start_values
    widths = [(0, 0)] * (values.ndim - 3) + [(1, 1)] * 3
    for repeat in range(SWEEPS):
        padded = jnp.pad(values, widths, mode='edge')
        earlier = [padded[..., :-2, 1:-1, 1:-1], padded[..., 1:-1, :-2, 1:-1], padded[..., 1:-1, 1:-1, :-2]]
        further = [padded[..., 2:, 1:-1, 1:-1], padded[..., 1:-1, 2:, 1:-1], padded[..., 1:-1, 1:-1, 2:]]
        growing, shrinking = godunov(values, earlier, further)
        values = values - pseudo_step * sign_field * (jnp.sqrt(jnp.where(sign_field > 0.0, growing, shrinking)) - 1.0)
    return values

def reference(level_set, displacement_prev, traction, load_mask, support_mask, extension, tile_count, tile_list):
    padded_phi = jnp.pad(level_set, 1)
    padded_e = stiffness(padded_phi)
    centre_e = padded_e[1:-1, 1:-1, 1:-1]
    weights = face_weights(padded_e)
    diagonal = weights[0]
    for weight in weights[1:]:
        diagonal = diagonal + weight
    diagonal = diagonal + coupling * centre_e
    free_cells = (1 - support_mask).astype(jnp.float32)
    force = traction[:, None, None, None] * load_mask.astype(jnp.float32)[None]
    moving = displacement_prev * free_cells[None]
    rim = ((0, 0), (1, 1), (1, 1), (1, 1))
    for repeat in range(JACOBI):
        image = operate(jnp.pad(moving, rim), weights, centre_e)
        moving = (moving + relax * (force - image) / diagonal[None]) * free_cells[None]
    image = operate(jnp.pad(moving, rim), weights, centre_e)
    energy = lax.optimization_barrier(jnp.sum(moving * image, axis=0))
    slope = 0.5 * (1.0 - jnp.square(jnp.tanh(level_set)))
    sensitivity = (slope * energy).astype(jnp.bfloat16)
    velocity = jnp.einsum('yk,xkz->xyz', extension.astype(jnp.float32), sensitivity.astype(jnp.float32))
    speed = velocity / (1.0 + jnp.abs(velocity))
    earlier = [padded_phi[:-2, 1:-1, 1:-1], padded_phi[1:-1, :-2, 1:-1], padded_phi[1:-1, 1:-1, :-2]]
    further = [padded_phi[2:, 1:-1, 1:-1], padded_phi[1:-1, 2:, 1:-1], padded_phi[1:-1, 1:-1, 2:]]
    growing, shrinking = godunov(level_set, earlier, further)
    advanced = level_set - advance_step * (jnp.maximum(speed, 0.0) * jnp.sqrt(growing) + jnp.minimum(speed, 0.0) * jnp.sqrt(shrinking))
    tiles_x, tiles_y, tiles_z = (CX // TILE, CY // TILE, CZ // TILE)
    counts = tile_count.reshape(N_GX, N_GY, N_GA)
    lists = tile_list.reshape(N_GX, N_GY, N_GA, TPD)
    entries = jnp.arange(TPD)
    usable = entries[None, None, None, :] < counts[..., None]
    chosen = (lists[..., :, None] == entries[None, None, None, None, :]) & usable[..., :, None]
    listed = jnp.any(chosen, axis=3)
    listed = listed.reshape(N_GX, N_GY, N_GA, tiles_x, tiles_y, tiles_z).transpose(0, 3, 1, 4, 2, 5)
    listed = listed.reshape(N_GX * tiles_x, N_GY * tiles_y, N_GA * tiles_z)
    split = advanced.reshape(NX // TILE, TILE, NY // TILE, TILE, NZ // TILE, TILE).transpose(0, 2, 4, 1, 3, 5)
    smoothed = reinit_tiles(split)
    merged = jnp.where(listed[..., None, None, None], smoothed, split)
    level_set_new = merged.transpose(0, 3, 1, 4, 2, 5).reshape(NX, NY, NZ)
    return (moving, level_set_new)
```

```python
import jax
import jax.numpy as jnp
from jax import lax
from jax.experimental import pallas as pl
from jax.experimental.pallas import tpu as pltpu
from jax.sharding import PartitionSpec as P

TILE = 32
SWEEPS = 4
RELAX = 0.6
ADVANCE = 0.5
PSEUDO = 0.3
CX, CY, CZ = 32, 32, 256
NY = 256
ROWS = CX * CY
LANES = 128
CHUNK = 8
UNROLL = 3
TINY = 1e-37
F32, BF16 = jnp.float32, jnp.bfloat16
LIMIT = 8 << 20


SWAP_NEAR = [(i, i ^ 1) for i in range(8)]
SWAP_FAR = [(1, 2), (2, 1), (3, 4), (4, 3), (5, 6), (6, 5), (7, 0), (0, 7)]
SWAP_Z = [(0, 1), (1, 0)]

VM = pl.BlockSpec(memory_space=pltpu.VMEM)
SM = pl.BlockSpec(memory_space=pltpu.SMEM)
ANY = pl.BlockSpec(memory_space=pltpu.HBM)
HALVES = (slice(0, LANES), slice(LANES, 2 * LANES))


def shape(*dims, dtype=F32):
    return jax.ShapeDtypeStruct(dims, dtype)


def call(kernel, outs, scratch, args, specs=None, out_specs=None):
    return pl.pallas_call(
        kernel,
        out_shape=outs,
        in_specs=specs or [VM] * len(args),
        out_specs=out_specs or [VM] * len(outs),
        scratch_shapes=scratch,
        compiler_params=pltpu.CompilerParams(vmem_limit_bytes=LIMIT),
    )(*args)


class Place:
    def __init__(self):
        gx, gy, ga = lax.axis_index("gx"), lax.axis_index("gy"), lax.axis_index("ga")
        self.even_x, self.even_y = gx % 2 == 0, gy % 2 == 0
        self.x_lo = (gx > 0).astype(F32)
        self.x_hi = (gx < lax.axis_size("gx") - 1).astype(F32)
        self.y_lo = (gy > 0).astype(F32)
        self.y_hi = (gy < lax.axis_size("gy") - 1).astype(F32)
        self.first_z = ga == 0
        self.z_hi = (ga == 0).astype(F32)
        self.z_lo = (ga != 0).astype(F32)


def rows(x):
    return pl.ds(pl.multiple_of(x * CY, CY), CY)


def load(ref, x, half, *lead):
    return ref[(*lead, half, rows(x), slice(None))].reshape(4, 8, LANES)


def store(ref, x, half, value, *lead):
    ref[(*lead, half, rows(x), slice(None))] = value.reshape(CY, LANES)


def load_natural(ref, x, half, *lead):
    parts = [ref[(*lead, half, x, pl.ds(r, 8, stride=4), slice(None))] for r in range(4)]
    return jnp.stack([part.reshape(8, LANES) for part in parts])


def store_natural(ref, x, half, value, *lead):
    for r in range(4):
        ref[(*lead, half, x, pl.ds(r, 8, stride=4), slice(None))] = value[r]


def small_iotas():
    sub = lax.broadcasted_iota(jnp.int32, (8, LANES), 0)
    lane = lax.broadcasted_iota(jnp.int32, (4, 8, LANES), 2)
    return sub, lane


def y_sides(sub, tile, low, high):
    first = jnp.where(sub == 0, low, pltpu.roll(tile[3], 1, 0))
    last = jnp.where(sub == 7, high, pltpu.roll(tile[0], 7, 0))
    below = jnp.concatenate([first[None], tile[:3]], axis=0)
    above = jnp.concatenate([tile[1:], last[None]], axis=0)
    return below, above


def z_sides(lane, tiles, low, high):
    down = [pltpu.roll(tile, 1, 2) for tile in tiles]
    up = [pltpu.roll(tile, LANES - 1, 2) for tile in tiles]
    below = [jnp.where(lane == 0, low, down[0]), jnp.where(lane == 0, down[0], down[1])]
    above = [
        jnp.where(lane == LANES - 1, up[1], up[0]),
        jnp.where(lane == LANES - 1, high, up[1]),
    ]
    return below, above


def column(place, zh, index):
    target = jnp.where(place.first_z, LANES - 1, 0)
    return pltpu.roll(zh, lax.rem(target - index + 256, LANES), 1).reshape(4, 8, LANES)


def emit_faces(place, fields, xs, ys, zs):
    near_x = jnp.where(place.even_x, CX - 1, 0)
    near_y = jnp.where(place.even_y, CY - 1, 0)
    edge = jnp.where(place.first_z, 1, 0)
    source = jnp.where(place.first_z, LANES - 1, 0)
    for c, (ref, lead) in enumerate(fields):
        for turn in range(2):
            x = near_x if turn == 0 else CX - 1 - near_x
            y = near_y if turn == 0 else CY - 1 - near_y
            for half in range(2):
                plane = ref[(*lead, half, rows(x), slice(None))]
                side = ref[(*lead, half, pl.ds(y, CX, stride=CY), slice(None))]
                xs[turn][c, :, HALVES[half]] = plane.astype(BF16)
                ys[turn][c, :, HALVES[half]] = side.astype(BF16)
    lane = lax.broadcasted_iota(jnp.int32, (CY, LANES), 1)

    def step(block, total):
        for k in range(4):
            x = block * 4 + k
            for c, (ref, lead) in enumerate(fields):
                tile = ref[(*lead, edge, rows(x), slice(None))]
                index = c * CX + x
                moved = pltpu.roll(tile, lax.rem(index - source + LANES, LANES), 1)
                total = jnp.where(lane == index, moved, total)
        return total

    zs[...] = lax.fori_loop(0, CX // 4, step, jnp.zeros((CY, LANES), F32)).astype(BF16)


def stage_halos(place, rx, ry, xh, yh, count):
    for c in range(count):
        near, far = rx[0][c].astype(F32), rx[1][c].astype(F32)
        xh[0, c] = jnp.where(place.even_x, far, near)
        xh[1, c] = jnp.where(place.even_x, near, far)
        near, far = ry[0][c].astype(F32), ry[1][c].astype(F32)
        low, high = jnp.where(place.even_y, far, near), jnp.where(place.even_y, near, far)
        for h, half in enumerate(HALVES):
            yh[0, c, h] = low[:, half]
            yh[1, c, h] = high[:, half]


def plane_of(ref, *lead):
    return [ref[(*lead, slice(None), half)].reshape(4, 8, LANES) for half in HALVES]


def planes(ref, x, *lead):
    return [load(ref, x, half, *lead) for half in range(2)]


def over_planes(step, below_end, above_end, within):
    step(0, below_end, lambda c: within(c, 1))

    def inner(block, carry):
        for k in range(UNROLL):
            x = 1 + block * UNROLL + k
            step(x, lambda c: within(c, x - 1), lambda c: within(c, x + 1))
        return carry

    lax.fori_loop(0, (CX - 2) // UNROLL, inner, 0)
    step(CX - 1, lambda c: within(c, CX - 2), above_end)


def pack_kernel(
    prev, level, support, u0, lev, free, xs1, xs2, ys1, ys2, zs, prev_in, level_in, support_in, sems
):
    place = Place()
    copies = []
    for i in range(CX // CHUNK):
        part, trio = pl.ds(i * CHUNK, CHUNK), []
        for h, half in enumerate(HALVES):
            pairs = [(prev.at[c, part, :, half], prev_in.at[c, h, part]) for c in range(3)]
            pairs.append((level.at[part, :, half], level_in.at[h, part]))
            pairs.append((support.at[part, :, half], support_in.at[h, part]))
            for source, target in pairs:
                sem = sems.at[i, len(trio)]
                trio.append(pltpu.make_async_copy(source, target, sem))
        copies.append(trio)
    for trio in copies:
        for one in trio:
            one.start()
    for i, trio in enumerate(copies):
        for one in trio:
            one.wait()

        def step(block, carry):
            for k in range(2):
                x = i * CHUNK + block * 2 + k
                for half in range(2):
                    keep = (1 - load_natural(support_in, x, half)).astype(F32)
                    store(free, x, half, keep)
                    store(lev, x, half, load_natural(level_in, x, half))
                    for c in range(3):
                        store(u0, x, half, load_natural(prev_in, x, half, c) * keep, c)
            return carry

        lax.fori_loop(0, CHUNK // 2, step, 0)
    fields = [(u0, (c,)) for c in range(3)] + [(lev, ())]
    emit_faces(place, fields, (xs1, xs2), (ys1, ys2), zs)


def prepare_kernel(lev, load_mask, extension, tanh, loaded, turned, load_in, sem):
    copies = [
        pltpu.make_async_copy(load_mask.at[:, :, half], load_in.at[h], sem.at[h])
        for h, half in enumerate(HALVES)
    ]
    for one in copies:
        one.start()

    def bend(block, carry):
        for k in range(2):
            for half in range(2):
                x = block * 2 + k
                store(tanh, x, half, jnp.tanh(load(lev, x, half)))
        return carry

    lax.fori_loop(0, CX // 2, bend, 0)
    for one in copies:
        one.wait()

    def turn(block, carry):
        for k in range(2):
            x = block * 2 + k
            for half in range(2):
                store(loaded, x, half, load_natural(load_in, x, half).astype(F32))
        return carry

    lax.fori_loop(0, CX // 2, turn, 0)

    def order(size, along):
        place = lax.broadcasted_iota(jnp.int32, (size, size), along)
        other = lax.broadcasted_iota(jnp.int32, (size, size), 1 - along)
        source = place // CY * CY + place % 8 * 4 + place // 8 % 4
        return (source == other).astype(BF16)

    held = jnp.dot(order(CY, 0), extension[...], preferred_element_type=F32).astype(BF16)
    held = jnp.dot(held, order(NY, 1), preferred_element_type=F32)
    turned[...] = held.astype(BF16)


def sum_sides(place, sub, lane, x, u, yh, zh, x_below, x_above, weights):
    xl, xu, yl, yu, zl, zu = weights
    found = []
    for c in range(3):
        tiles = planes(u, x, c)
        side = column(place, zh, c * CX + x)
        z_below, z_above = z_sides(lane, tiles, side, side)
        x_lo, x_hi = x_below(c), x_above(c)
        sums = []
        for half in range(2):
            low, high = (yh[side, c, half, pl.ds(x, 8, stride=0), :] for side in range(2))
            y_below, y_above = y_sides(sub, tiles[half], low, high)
            total = xl[half] * x_lo[half] + xu[half] * x_hi[half]
            total = total + (yl[half] * y_below + yu[half] * y_above)
            total = total + (zl[half] * z_below[half] + zu[half] * z_above[half])
            sums.append(total)
        found.append((tiles, sums))
    return found


def first_kernel(
    traction, u, lev, free, tanh, loaded, rx1, rx2, ry1, ry2, rz,
    new, xs1, xs2, ys1, ys2, zs, wx, wyl, wyh, wzl, wzh, coup, diag, gain,
    xh, yh, zh,
):
    place = Place()
    sub, lane = small_iotas()
    stage_halos(place, (rx1, rx2), (ry1, ry2), xh, yh, 4)
    zh[0] = rz[...].astype(F32)
    bent = jnp.tanh(zh[0])
    zh[1] = bent * place.z_lo
    zh[2] = bent * place.z_hi
    yh[0, 3] = jnp.tanh(yh[0, 3]) * place.y_lo
    yh[1, 3] = jnp.tanh(yh[1, 3]) * place.y_hi
    xh[0, 3] = jnp.tanh(xh[0, 3]) * place.x_lo
    xh[1, 3] = jnp.tanh(xh[1, 3]) * place.x_hi
    row_mask = lax.broadcasted_iota(jnp.int32, (4, 8, LANES), 0) * 8 + sub[None]
    y_low = jnp.where(row_mask == 0, place.y_lo, 1.0)
    y_high = jnp.where(row_mask == CY - 1, place.y_hi, 1.0)
    z_low = [jnp.where(lane == 0, place.z_lo, 1.0), 1.0]
    z_high = [1.0, jnp.where(lane == LANES - 1, place.z_hi, 1.0)]

    def weight(a, b):
        return 0.525 + 0.2375 * (a + b)

    def step(x, x_below, x_above):
        centre = planes(tanh, x)
        z_below, z_above = z_sides(
            lane, centre, column(place, zh[1], 96 + x), column(place, zh[2], 96 + x)
        )
        t_below, t_above = x_below(3), x_above(3)
        kept, factors, totals, halves, forces = [[], [], [], [], [], []], [], [], [], []
        for half in range(2):
            mid = centre[half]
            low, high = (yh[side, 3, half, pl.ds(x, 8, stride=0), :] for side in range(2))
            y_below, y_above = y_sides(sub, mid, low, high)
            xl, xu = weight(mid, t_below[half]), weight(mid, t_above[half])
            yl, yu = weight(mid, y_below), weight(mid, y_above)
            zl, zu = weight(mid, z_below[half]), weight(mid, z_above[half])
            total = (xl + xu) + (yl + yu) + (zl + zu)
            middle = 0.2625 + 0.2375 * mid
            factor = RELAX * load(free, x, half) / (total + middle)
            yl, yu = yl * y_low, yu * y_high
            zl, zu = zl * z_low[half], zu * z_high[half]
            if isinstance(x, int) and x == 0:
                xl = xl * place.x_lo
                store(wx, 0, half, xl)
            if isinstance(x, int) and x == CX - 1:
                xu = xu * place.x_hi
            store(wx, x + 1, half, xu)
            store(wyl, x, half, yl)
            store(wyh, x, half, yu)
            store(wzl, x, half, zl)
            store(wzh, x, half, zu)
            store(coup, x, half, middle)
            store(diag, x, half, total)
            store(gain, x, half, factor)
            for into, one in zip(kept, (xl, xu, yl, yu, zl, zu)):
                into.append(one)
            factors.append(factor)
            totals.append(total)
            halves.append(middle)
            forces.append(load(loaded, x, half))
        found = sum_sides(place, sub, lane, x, u, yh, zh[0], x_below, x_above, kept)
        for half in range(2):
            shared = halves[half] * (found[0][0][half] + found[1][0][half] + found[2][0][half])
            for c in range(3):
                tile, near = found[c][0][half], found[c][1][half]
                push = near - shared + traction[c] * forces[half] - totals[half] * tile
                store(new, x, half, tile + factors[half] * push, c)

    over_planes(
        step,
        lambda c: plane_of(xh, 0, c),
        lambda c: plane_of(xh, 1, c),
        lambda c, x: planes(tanh, x) if c == 3 else planes(u, x, c),
    )
    emit_faces(place, [(new, (c,)) for c in range(3)], (xs1, xs2), (ys1, ys2), zs)


def sweep_kernel(
    traction, u, wx, wyl, wyh, wzl, wzh, coup, diag, gain, loaded, rx1, rx2, ry1, ry2, rz,
    new, xs1, xs2, ys1, ys2, zs, xh, yh, zh,
):
    place = Place()
    sub, lane = small_iotas()
    stage_halos(place, (rx1, rx2), (ry1, ry2), xh, yh, 3)
    zh[...] = rz[...].astype(F32)

    def step(x, x_below, x_above):
        weights = [planes(wx, x), planes(wx, x + 1)]
        weights += [planes(ref, x) for ref in (wyl, wyh, wzl, wzh)]
        found = sum_sides(place, sub, lane, x, u, yh, zh[...], x_below, x_above, weights)
        for half in range(2):
            shared = found[0][0][half] + found[1][0][half] + found[2][0][half]
            shared = load(coup, x, half) * shared
            factor, force, total = (load(ref, x, half) for ref in (gain, loaded, diag))
            for c in range(3):
                tile, near = found[c][0][half], found[c][1][half]
                push = near - shared + traction[c] * force - total * tile
                store(new, x, half, tile + factor * push, c)

    over_planes(
        step,
        lambda c: plane_of(xh, 0, c),
        lambda c: plane_of(xh, 1, c),
        lambda c, x: planes(u, x, c),
    )
    emit_faces(place, [(new, (c,)) for c in range(3)], (xs1, xs2), (ys1, ys2), zs)


def energy_kernel(
    u, tanh, wx, wyl, wyh, wzl, wzh, coup, diag, extension, rx1, rx2, ry1, ry2, rz,
    out, xh, yh, zh,
):
    place = Place()
    sub, lane = small_iotas()
    stage_halos(place, (rx1, rx2), (ry1, ry2), xh, yh, 3)
    zh[...] = rz[...].astype(F32)

    def step(x, x_below, x_above):
        weights = [planes(wx, x), planes(wx, x + 1)]
        weights += [planes(ref, x) for ref in (wyl, wyh, wzl, wzh)]
        found = sum_sides(place, sub, lane, x, u, yh, zh[...], x_below, x_above, weights)
        for half in range(2):
            shared = found[0][0][half] + found[1][0][half] + found[2][0][half]
            shared = load(coup, x, half) * shared
            total = load(diag, x, half)
            energy = jnp.zeros((4, 8, LANES), F32)
            for c in range(3):
                tile, near = found[c][0][half], found[c][1][half]
                energy = energy + tile * (total * tile + shared - near)
            bent = load(tanh, x, half)
            value = 0.5 * (1.0 - bent * bent) * energy
            out[x + x // 4, :, HALVES[half]] = value.reshape(CY, LANES).astype(BF16)

    over_planes(
        step,
        lambda c: plane_of(xh, 0, c),
        lambda c: plane_of(xh, 1, c),
        lambda c, x: planes(u, x, c),
    )
    for part in range(8):
        out[5 * part + 4] = extension[...]


def unpack_kernel(u, out, natural, sems):
    copies = []
    for c in range(3):

        def step(block, carry):
            for k in range(2):
                x = block * 2 + k
                for half in range(2):
                    store_natural(natural, x, half, load(u, x, half, c), c)
            return carry

        lax.fori_loop(0, CX // 2, step, 0)
        for h, half in enumerate(HALVES):
            one = pltpu.make_async_copy(natural.at[c, h], out.at[c, :, :, half], sems.at[c, h])
            one.start()
            copies.append(one)
    for one in copies:
        one.wait()


def product_kernel(received, out):
    matrix = jnp.concatenate([received[5 * part + 4] for part in range(8)], axis=0)
    for x in range(4):
        field = jnp.concatenate([received[5 * part + x] for part in range(8)], axis=0)
        moved = jnp.dot(matrix, field, preferred_element_type=F32).astype(BF16)
        for part in range(8):
            out[4 * part + x] = moved[CY * part : CY * (part + 1)]


def slopes_kernel(lev, rx1, rx2, ry1, ry2, rz, grow, shrink, xh, yh, zh):
    place = Place()
    sub, lane = small_iotas()
    near, far = rx1[3].astype(F32), rx2[3].astype(F32)
    xh[0] = jnp.where(place.even_x, far, near) * place.x_lo
    xh[1] = jnp.where(place.even_x, near, far) * place.x_hi
    near, far = ry1[3].astype(F32), ry2[3].astype(F32)
    low = jnp.where(place.even_y, far, near) * place.y_lo
    high = jnp.where(place.even_y, near, far) * place.y_hi
    for h, half in enumerate(HALVES):
        yh[0, h] = low[:, half]
        yh[1, h] = high[:, half]
    zh[0] = rz[...].astype(F32) * place.z_lo
    zh[1] = rz[...].astype(F32) * place.z_hi

    def step(x, x_below, x_above):
        centre = planes(lev, x)
        z_below, z_above = z_sides(
            lane, centre, column(place, zh[0], 96 + x), column(place, zh[1], 96 + x)
        )
        x_lo, x_hi = x_below(0), x_above(0)
        for half in range(2):
            mid = centre[half]
            low, high = (yh[side, half, pl.ds(x, 8, stride=0), :] for side in range(2))
            y_below, y_above = y_sides(sub, mid, low, high)
            growing = jnp.zeros((4, 8, LANES), F32)
            shrinking = jnp.zeros((4, 8, LANES), F32)
            pairs = ((x_lo[half], x_hi[half]), (y_below, y_above), (z_below[half], z_above[half]))
            for below, above in pairs:
                up = jnp.maximum(mid - jnp.minimum(below, above), 0.0)
                down = jnp.maximum(jnp.maximum(below, above) - mid, 0.0)
                growing = growing + up * up
                shrinking = shrinking + down * down
            store(grow, x, half, jnp.sqrt(growing))
            store(shrink, x, half, jnp.sqrt(shrinking))

    over_planes(
        step,
        lambda c: plane_of(xh, 0),
        lambda c: plane_of(xh, 1),
        lambda c, x: planes(lev, x),
    )


def final_kernel(
    counts, listing, lev, velocity, grow, shrink, out, first, second, sign, natural, sems
):
    gx, gy, ga = lax.axis_index("gx"), lax.axis_index("gy"), lax.axis_index("ga")
    sub, lane = small_iotas()
    own = counts[gx, gy * lax.axis_size("ga") + ga]
    listed = []
    for half in range(2):
        tile = lane[0] // TILE + half * (LANES // TILE)
        mask = jnp.zeros((8, LANES), F32)
        for entry in range(CZ // TILE):
            hit = jnp.where(entry < own, listing[0, entry], -1)
            mask = jnp.where(tile == hit, PSEUDO, mask)
        listed.append(mask)
    low_z, high_z = lane % TILE == 0, lane % TILE == TILE - 1

    def advance(block, carry):
        for k in range(2):
            x = block * 2 + k
            for half in range(2):
                moved = velocity[x, :, HALVES[half]].astype(F32).reshape(4, 8, LANES)
                speed = moved / (1.0 + jnp.abs(moved))
                change = jnp.maximum(speed, 0.0) * load(grow, x, half)
                change = change + jnp.minimum(speed, 0.0) * load(shrink, x, half)
                value = load(lev, x, half) - ADVANCE * change
                store(first, x, half, value)
                scaled = listed[half] * (value / jnp.sqrt(value * value + 1.0))
                store(sign, x, half, scaled)
        return carry

    lax.fori_loop(0, CX // 2, advance, 0)

    def sweep(source, x):
        done = []
        for half in range(2):
            centre = load(source, x, half)
            strength = load(sign, x, half)
            way = jnp.where(strength > 0.0, 1.0, -1.0)
            y_below, y_above = y_sides(sub, centre, centre[0], centre[3])
            sides = (
                (
                    load(source, jnp.maximum(x - 1, 0), half),
                    load(source, jnp.minimum(x + 1, CX - 1), half),
                ),
                (y_below, y_above),
                (
                    jnp.where(low_z, centre, pltpu.roll(centre, 1, 2)),
                    jnp.where(high_z, centre, pltpu.roll(centre, LANES - 1, 2)),
                ),
            )
            faced = way * centre
            total = None
            for below, above in sides:
                rise = jnp.maximum(faced - jnp.minimum(way * below, way * above), 0.0)
                total = rise * rise if total is None else total + rise * rise
            root = total * lax.rsqrt(jnp.maximum(total, TINY))
            done.append(centre - strength * (root - 1.0))
        return done

    buffers = [first, second]
    for turn in range(SWEEPS - 1):
        source, target = buffers[turn % 2], buffers[(turn + 1) % 2]

        def step(block, carry):
            for k in range(2):
                x = block * 2 + k
                for half, value in enumerate(sweep(source, x)):
                    store(target, x, half, value)
            return carry

        lax.fori_loop(0, CX // 2, step, 0)
    source = buffers[(SWEEPS - 1) % 2]
    copies = []
    for i in range(CX // CHUNK):

        def last(block, carry):
            for k in range(2):
                x = i * CHUNK + block * 2 + k
                for half, value in enumerate(sweep(source, x)):
                    store_natural(natural, x, half, value)
            return carry

        lax.fori_loop(0, CHUNK // 2, last, 0)
        part = pl.ds(i * CHUNK, CHUNK)
        for h, half in enumerate(HALVES):
            one = pltpu.make_async_copy(natural.at[h, part], out.at[part, :, half], sems.at[i, h])
            one.start()
            copies.append(one)
    for one in copies:
        one.wait()


def exchange(xs1, xs2, ys1, ys2, zs):
    return (
        lax.ppermute(xs1, "gx", SWAP_NEAR),
        lax.ppermute(xs2, "gx", SWAP_FAR),
        lax.ppermute(ys1, "gy", SWAP_NEAR),
        lax.ppermute(ys2, "gy", SWAP_FAR),
        lax.ppermute(zs, "ga", SWAP_Z),
    )


def faces(count):
    return [shape(count, 32, CZ, dtype=BF16)] * 4 + [shape(CY, LANES, dtype=BF16)]


def halo_scratch(count):
    return [pltpu.VMEM((2, count, CY, CZ), F32), pltpu.VMEM((2, count, 2, CX, LANES), F32)]


def local(
    level_set, displacement_prev, traction, load_mask, support_mask, extension, tile_count, tile_list
):
    displacement_prev, level_set, support_mask, load_mask = (
        pltpu.with_memory_space_constraint(x, pltpu.HBM)
        for x in (displacement_prev, level_set, support_mask, load_mask)
    )
    flat = shape(2, ROWS, LANES)
    field = shape(3, 2, ROWS, LANES)
    column_scratch = pltpu.VMEM((CY, LANES), F32)
    u, lev, free, *sent = call(
        pack_kernel,
        [field, flat, flat] + faces(4),
        [
            pltpu.VMEM((3, 2, CX, CY, LANES), F32),
            pltpu.VMEM((2, CX, CY, LANES), F32),
            pltpu.VMEM((2, CX, CY, LANES), jnp.int32),
            pltpu.SemaphoreType.DMA((CX // CHUNK, 10)),
        ],
        (displacement_prev, level_set, support_mask),
        [ANY] * 3,
    )
    got = exchange(*sent)
    level_got = got
    tanh, loaded, turned = call(
        prepare_kernel,
        [flat] * 2 + [shape(CY, NY, dtype=BF16)],
        [pltpu.VMEM((2, CX, CY, LANES), jnp.int32), pltpu.SemaphoreType.DMA((2,))],
        (lev, load_mask, extension),
        [VM, ANY, VM],
    )
    u, *rest = call(
        first_kernel,
        [field] + faces(3) + [shape(2, ROWS + CY, LANES)] + [flat] * 7,
        halo_scratch(4) + [pltpu.VMEM((3, CY, LANES), F32)],
        (traction, u, lev, free, tanh, loaded, *got),
        [SM] + [VM] * 10,
    )
    sent, made = rest[:5], rest[5:]
    got = exchange(*sent)
    grow, shrink = call(
        slopes_kernel, [flat] * 2,
        [pltpu.VMEM((2, CY, CZ), F32), pltpu.VMEM((2, 2, CX, LANES), F32)]
        + [pltpu.VMEM((2, CY, LANES), F32)],
        (lev, *level_got),
    )
    for turn in range(2):
        u, *sent = call(
            sweep_kernel, [field] + faces(3), halo_scratch(3) + [column_scratch],
            (traction, u, *made, loaded, *got),
            [SM] + [VM] * (len(made) + 7),
        )
        got = exchange(*sent)
    (displacement,) = call(
        unpack_kernel, [shape(3, CX, CY, CZ)],
        [pltpu.VMEM((3, 2, CX, CY, LANES), F32), pltpu.SemaphoreType.DMA((3, 2))],
        (u,), None, [ANY],
    )
    (sensitivity,) = call(
        energy_kernel, [shape(40, CY, CZ, dtype=BF16)], halo_scratch(3) + [column_scratch],
        (u, tanh, *made[:7], turned, *got),
    )
    sensitivity = lax.all_to_all(sensitivity, "gy", split_axis=0, concat_axis=0, tiled=True)
    (velocity,) = call(product_kernel, [shape(CX, CY, CZ, dtype=BF16)], [], (sensitivity,))
    velocity = lax.all_to_all(velocity, "gy", split_axis=0, concat_axis=0, tiled=True)
    (level_new,) = call(
        final_kernel, [shape(CX, CY, CZ)],
        [pltpu.VMEM((2, ROWS, LANES), F32)] * 3
        + [pltpu.VMEM((2, CX, CY, LANES), F32), pltpu.SemaphoreType.DMA((CX // CHUNK, 2))],
        (tile_count, tile_list, lev, velocity, grow, shrink),
        [SM, SM] + [VM] * 4,
        [ANY],
    )
    return (displacement, level_new)


def solution(mesh):
    return jax.shard_map(
        local,
        mesh=mesh,
        in_specs=(
            P("gx", "gy", "ga"),
            P(None, "gx", "gy", "ga"),
            P(),
            P("gx", "gy", "ga"),
            P("gx", "gy", "ga"),
            P("gy", None),
            P(),
            P(("gx", "gy", "ga"), None),
        ),
        out_specs=(P(None, "gx", "gy", "ga"), P("gx", "gy", "ga")),
        check_vma=False,
    )
```

```python
import jax
import jax.numpy as jnp
from jax import lax
from jax.experimental import pallas as pl
from jax.experimental.pallas import tpu as pltpu
from jax.sharding import PartitionSpec as P

TILE = 32
SWEEPS = 4
RELAX = 0.6
ADVANCE = 0.5
PSEUDO = 0.3
CX, CY, CZ = 32, 32, 256
NY = 256
ROWS = CX * CY
LANES = 128
CHUNK = 8
UNROLL = 5
TINY = 1e-37
F32, BF16 = jnp.float32, jnp.bfloat16
LIMIT = 10 << 20


SWAP_NEAR = [(i, i ^ 1) for i in range(8)]
SWAP_FAR = [(1, 2), (2, 1), (3, 4), (4, 3), (5, 6), (6, 5), (7, 0), (0, 7)]
SWAP_Z = [(0, 1), (1, 0)]

VM = pl.BlockSpec(memory_space=pltpu.VMEM)
SM = pl.BlockSpec(memory_space=pltpu.SMEM)
ANY = pl.BlockSpec(memory_space=pltpu.HBM)
LOOSE = pl.BlockSpec(memory_space=pl.ANY)
CELLS = [(half, r) for r in range(4) for half in range(2)]
HALVES = (slice(0, LANES), slice(LANES, 2 * LANES))


def shape(*dims, dtype=F32):
    return jax.ShapeDtypeStruct(dims, dtype)


def call(kernel, outs, scratch, args, specs=None, out_specs=None):
    return pl.pallas_call(
        kernel,
        out_shape=outs,
        in_specs=specs or [VM] * len(args),
        out_specs=out_specs or [VM] * len(outs),
        scratch_shapes=scratch,
        compiler_params=pltpu.CompilerParams(vmem_limit_bytes=LIMIT),
    )(*args)


class Place:
    def __init__(self):
        gx, gy, ga = lax.axis_index("gx"), lax.axis_index("gy"), lax.axis_index("ga")
        self.even_x, self.even_y = gx % 2 == 0, gy % 2 == 0
        self.x_lo = (gx > 0).astype(F32)
        self.x_hi = (gx < lax.axis_size("gx") - 1).astype(F32)
        self.y_lo = (gy > 0).astype(F32)
        self.y_hi = (gy < lax.axis_size("gy") - 1).astype(F32)
        self.first_z = ga == 0
        self.z_hi = (ga == 0).astype(F32)
        self.z_lo = (ga != 0).astype(F32)


def rows(x):
    return pl.ds(pl.multiple_of(x * CY, CY), CY)


def load(ref, x, half, r, *lead):
    start = pl.multiple_of(x * CY + r * 8, 8)
    return ref[(*lead, half, pl.ds(start, 8), slice(None))]


def store(ref, x, half, r, value, *lead):
    start = pl.multiple_of(x * CY + r * 8, 8)
    ref[(*lead, half, pl.ds(start, 8), slice(None))] = value


def load_natural(ref, x, half, r, *lead):
    return ref[(*lead, half, x, pl.ds(r, 8, stride=4), slice(None))]


def store_natural(ref, x, half, r, value, *lead):
    ref[(*lead, half, x, pl.ds(r, 8, stride=4), slice(None))] = value


def small_iotas():
    sub = lax.broadcasted_iota(jnp.int32, (8, LANES), 0)
    lane = lax.broadcasted_iota(jnp.int32, (8, LANES), 1)
    return sub, lane


def y_sides(sub, r, get, low, high):
    below = get(r - 1) if r else jnp.where(sub == 0, low(), pltpu.roll(get(3), 1, 0))
    above = get(r + 1) if r < 3 else jnp.where(sub == 7, high(), pltpu.roll(get(0), 7, 0))
    return below, above


def z_sides(lane, tiles, low, high):
    down = [pltpu.roll(tile, 1, 1) for tile in tiles]
    up = [pltpu.roll(tile, LANES - 1, 1) for tile in tiles]
    below = [jnp.where(lane == 0, low, down[0]), jnp.where(lane == 0, down[0], down[1])]
    above = [
        jnp.where(lane == LANES - 1, up[1], up[0]),
        jnp.where(lane == LANES - 1, high, up[1]),
    ]
    return below, above


def column(place, zh, index):
    target = jnp.where(place.first_z, LANES - 1, 0)
    return pltpu.roll(zh, lax.rem(target - index + 256, LANES), 1)


STEP = CX + 1


def keep_rows(strips, c, x, half, r, value):
    if r == 0:
        strips[c, 0, half, pl.ds(x, 8, stride=STEP), :] = value
    if r == 3:
        strips[c, 1, half, pl.ds(x + 1, 8, stride=STEP), :] = value


def emit_faces(place, fields, strips, xs, ys):
    near_x = jnp.where(place.even_x, CX - 1, 0)
    last = 7 * STEP + 1
    for c, (ref, lead) in enumerate(fields):
        for half in range(2):
            for turn in range(2):
                x = near_x if turn == 0 else CX - 1 - near_x
                plane = ref[(*lead, half, rows(x), slice(None))]
                xs[turn][c, :, HALVES[half]] = plane.astype(BF16)
            low, high = strips[c, 0, half, 0:CX, :], strips[c, 1, half, last : last + CX, :]
            ys[0][c, :, HALVES[half]] = jnp.where(place.even_y, high, low).astype(BF16)
            ys[1][c, :, HALVES[half]] = jnp.where(place.even_y, low, high).astype(BF16)


def strip_scratch(count):
    return [pltpu.VMEM((count, 2, 2, 8 * STEP + 8, LANES), F32)]


class ZFace:
    def __init__(self, place):
        source = jnp.where(place.first_z, LANES - 1, 0)
        pick = lax.broadcasted_iota(jnp.int32, (LANES, LANES), 0) == source
        self.pick = jnp.where(pick, 1.0, 0.0).astype(BF16)
        self.lane = lax.broadcasted_iota(jnp.int32, (CY, LANES), 1)
        self.first_z = place.first_z

    def begin(self):
        return jnp.zeros((CY, LANES), F32)

    def add(self, total, x, edges):
        chosen = [
            jnp.where(self.first_z, high, low) for pairs in edges for low, high in pairs
        ]
        wide = jnp.concatenate(chosen, axis=0).astype(BF16)
        wide = jnp.dot(wide, self.pick, preferred_element_type=F32)
        for c in range(len(edges)):
            total = jnp.where(self.lane == c * CX + x, wide[c * CY : (c + 1) * CY], total)
        return total

    def whole(self, ref, group=8):
        edge = jnp.where(self.first_z, 1, 0)
        total = self.begin()
        for c in range(3):
            for block in range(CX // group):
                part = pl.ds(block * group * CY, group * CY)
                wide = ref[c, edge, part, :].astype(BF16)
                wide = jnp.dot(wide, self.pick, preferred_element_type=F32)
                for k in range(group):
                    hit = self.lane == c * CX + block * group + k
                    total = jnp.where(hit, wide[k * CY : (k + 1) * CY], total)
        return total


def stage_halos(place, rx, ry, xh, yh, count):
    for c in range(count):
        near, far = rx[0][c].astype(F32), rx[1][c].astype(F32)
        xh[0, c] = jnp.where(place.even_x, far, near)
        xh[1, c] = jnp.where(place.even_x, near, far)
        near, far = ry[0][c].astype(F32), ry[1][c].astype(F32)
        low, high = jnp.where(place.even_y, far, near), jnp.where(place.even_y, near, far)
        for h, half in enumerate(HALVES):
            yh[0, c, h] = low[:, half]
            yh[1, c, h] = high[:, half]


def over_planes(step, end, within):
    step(0, lambda *at: end(0, *at), lambda *at: within(1, *at))

    def inner(block, carry):
        for k in range(UNROLL):
            x = 1 + block * UNROLL + k
            step(x, lambda *at: within(x - 1, *at), lambda *at: within(x + 1, *at))
        return carry

    lax.fori_loop(0, (CX - 2) // UNROLL, inner, 0)
    step(CX - 1, lambda *at: within(CX - 2, *at), lambda *at: end(1, *at))


def halo_plane(xh, side, c, half, r):
    return xh[side, c, r * 8 : r * 8 + 8, HALVES[half]]


def pack_kernel(
    prev, level, support, u0, lev, free, xs1, xs2, ys1, ys2, zs, prev_in, level_in, support_in, sems,
    strips,
):
    place = Place()
    copies = []
    for i in range(CX // CHUNK):
        part, trio = pl.ds(i * CHUNK, CHUNK), []
        for h, half in enumerate(HALVES):
            pairs = [(prev.at[c, part, :, half], prev_in.at[c, h, part]) for c in range(3)]
            pairs.append((level.at[part, :, half], level_in.at[h, part]))
            pairs.append((support.at[part, :, half], support_in.at[h, part]))
            for source, target in pairs:
                sem = sems.at[i, len(trio)]
                trio.append(pltpu.make_async_copy(source, target, sem))
        copies.append(trio)
    for trio in copies:
        for one in trio:
            one.start()
    face = ZFace(place)
    total = face.begin()
    for i, trio in enumerate(copies):
        for one in trio:
            one.wait()

        def step(block, total):
            for k in range(4):
                x = i * CHUNK + block * 4 + k
                edges = [[], [], [], []]
                for r in range(4):
                    rows_of = [[], [], [], []]
                    for half in range(2):
                        keep = (1 - load_natural(support_in, x, half, r)).astype(F32)
                        store(free, x, half, r, keep)
                        for c in range(3):
                            value = load_natural(prev_in, x, half, r, c) * keep
                            store(u0, x, half, r, value, c)
                            keep_rows(strips, c, x, half, r, value)
                            rows_of[c].append(value)
                        value = load_natural(level_in, x, half, r)
                        store(lev, x, half, r, value)
                        keep_rows(strips, 3, x, half, r, value)
                        rows_of[3].append(value)
                    for c in range(4):
                        edges[c].append(rows_of[c])
                total = face.add(total, x, edges)
            return total

        total = lax.fori_loop(0, CHUNK // 4, step, total)
    fields = [(u0, (c,)) for c in range(3)] + [(lev, ())]
    emit_faces(place, fields, strips, (xs1, xs2), (ys1, ys2))
    zs[...] = total.astype(BF16)


def prepare_kernel(lev, load_mask, extension, tanh, loaded, turned, load_in, sem):
    copies = [
        pltpu.make_async_copy(load_mask.at[:, :, half], load_in.at[h], sem.at[h])
        for h, half in enumerate(HALVES)
    ]
    for one in copies:
        one.start()

    def bend(block, carry):
        for k in range(2):
            for half, r in CELLS:
                x = block * 2 + k
                store(tanh, x, half, r, jnp.tanh(load(lev, x, half, r)))
        return carry

    lax.fori_loop(0, CX // 2, bend, 0)
    for one in copies:
        one.wait()

    def turn(block, carry):
        for k in range(2):
            x = block * 2 + k
            for half, r in CELLS:
                store(loaded, x, half, r, load_natural(load_in, x, half, r).astype(F32))
        return carry

    lax.fori_loop(0, CX // 2, turn, 0)

    def order(size, along):
        place = lax.broadcasted_iota(jnp.int32, (size, size), along)
        other = lax.broadcasted_iota(jnp.int32, (size, size), 1 - along)
        source = place // CY * CY + place % 8 * 4 + place // 8 % 4
        return (source == other).astype(BF16)

    held = jnp.dot(order(CY, 0), extension[...], preferred_element_type=F32).astype(BF16)
    held = jnp.dot(held, order(NY, 1), preferred_element_type=F32)
    turned[...] = held.astype(BF16)


def sum_sides(place, sub, lane, x, r, u, yh, sides, x_below, x_above, weights):
    found = []
    for c in range(3):
        tiles = [load(u, x, half, r, c) for half in range(2)]
        side = sides[c][r * 8 : r * 8 + 8]
        z_below, z_above = z_sides(lane, tiles, side, side)
        sums = []
        for half in range(2):
            xl, xu, yl, yu, zl, zu = (weight[half] for weight in weights)
            y_below, y_above = y_sides(
                sub,
                r,
                lambda row: load(u, x, half, row, c),
                lambda: yh[0, c, half, pl.ds(x, 8, stride=0), :],
                lambda: yh[1, c, half, pl.ds(x, 8, stride=0), :],
            )
            total = xl * x_below(c, half, r) + xu * x_above(c, half, r)
            total = total + (yl * y_below + yu * y_above)
            total = total + (zl * z_below[half] + zu * z_above[half])
            sums.append(total)
        found.append((tiles, sums))
    return found


def columns(place, zh, x):
    return [column(place, zh, c * CX + x) for c in range(3)]


def stored_weights(x, r, wx, wyl, wyh, wzl, wzh):
    pairs = [(wx, x), (wx, x + 1), (wyl, x), (wyh, x), (wzl, x), (wzh, x)]
    return [[load(ref, at, half, r) for half in range(2)] for ref, at in pairs]


def first_kernel(
    traction, u, lev, free, tanh, loaded, rx1, rx2, ry1, ry2, rz,
    new, xs1, xs2, ys1, ys2, zs, wx, wyl, wyh, wzl, wzh, coup, diag, gain, keep, push,
    xh, yh, zh, strips,
):
    place = Place()
    sub, lane = small_iotas()
    stage_halos(place, (rx1, rx2), (ry1, ry2), xh, yh, 4)
    zh[0] = rz[...].astype(F32)
    bent = jnp.tanh(zh[0])
    zh[1] = bent * place.z_lo
    zh[2] = bent * place.z_hi
    yh[0, 3] = jnp.tanh(yh[0, 3]) * place.y_lo
    yh[1, 3] = jnp.tanh(yh[1, 3]) * place.y_hi
    xh[0, 3] = jnp.tanh(xh[0, 3]) * place.x_lo
    xh[1, 3] = jnp.tanh(xh[1, 3]) * place.x_hi
    y_low = jnp.where(sub == 0, place.y_lo, 1.0)
    y_high = jnp.where(sub == 7, place.y_hi, 1.0)
    z_low = jnp.where(lane == 0, place.z_lo, 1.0)
    z_high = jnp.where(lane == LANES - 1, place.z_hi, 1.0)

    def weight(a, b):
        return 0.525 + 0.2375 * (a + b)

    def step(x, x_below, x_above):
        low_side, high_side = column(place, zh[1], 96 + x), column(place, zh[2], 96 + x)
        sides = columns(place, zh[0], x)
        for r in range(4):
            part = slice(r * 8, r * 8 + 8)
            centre = [load(tanh, x, half, r) for half in range(2)]
            z_below, z_above = z_sides(lane, centre, low_side[part], high_side[part])
            kept, cells = [[], [], [], [], [], []], []
            for half in range(2):
                mid = centre[half]
                y_below, y_above = y_sides(
                    sub,
                    r,
                    lambda row: load(tanh, x, half, row),
                    lambda: yh[0, 3, half, pl.ds(x, 8, stride=0), :],
                    lambda: yh[1, 3, half, pl.ds(x, 8, stride=0), :],
                )
                xl, xu = weight(mid, x_below(3, half, r)), weight(mid, x_above(3, half, r))
                yl, yu = weight(mid, y_below), weight(mid, y_above)
                zl, zu = weight(mid, z_below[half]), weight(mid, z_above[half])
                total = (xl + xu) + (yl + yu) + (zl + zu)
                middle = 0.2625 + 0.2375 * mid
                factor = RELAX * load(free, x, half, r) / (total + middle)
                stay, force = 1.0 - factor * total, factor * load(loaded, x, half, r)
                if r == 0:
                    yl = yl * y_low
                if r == 3:
                    yu = yu * y_high
                if half == 0:
                    zl = zl * z_low
                else:
                    zu = zu * z_high
                if isinstance(x, int) and x == 0:
                    xl = xl * place.x_lo
                    store(wx, 0, half, r, xl)
                if isinstance(x, int) and x == CX - 1:
                    xu = xu * place.x_hi
                store(wx, x + 1, half, r, xu)
                stored = (wyl, yl), (wyh, yu), (wzl, zl), (wzh, zu), (coup, middle)
                stored += (diag, total), (gain, factor), (keep, stay), (push, force)
                for ref, value in stored:
                    store(ref, x, half, r, value)
                for into, one in zip(kept, (xl, xu, yl, yu, zl, zu)):
                    into.append(one)
                cells.append((middle, factor, stay, force))
            found = sum_sides(
                place, sub, lane, x, r, u, yh, sides, x_below, x_above, kept
            )
            update(traction, found, cells, x, r, new, strips)

    def end(side, c, half, r):
        return halo_plane(xh, side, c, half, r)

    def within(x, c, half, r):
        return load(tanh, x, half, r) if c == 3 else load(u, x, half, r, c)

    over_planes(step, end, within)
    emit_faces(place, [(new, (c,)) for c in range(3)], strips, (xs1, xs2), (ys1, ys2))
    zs[...] = ZFace(place).whole(new).astype(BF16)


def update(traction, found, cells, x, r, new, strips):
    for half in range(2):
        middle, factor, stay, force = cells[half]
        shared = middle * (found[0][0][half] + found[1][0][half] + found[2][0][half])
        for c in range(3):
            tile, near = found[c][0][half], found[c][1][half]
            value = stay * tile + factor * (near - shared) + traction[c] * force
            store(new, x, half, r, value, c)
            keep_rows(strips, c, x, half, r, value)


def sweep_kernel(
    traction, u, wx, wyl, wyh, wzl, wzh, coup, diag, gain, keep, push, rx1, rx2, ry1, ry2, rz, held,
    new, xs1, xs2, ys1, ys2, zs, xh, yh, zh, strips,
):
    place = Place()
    sub, lane = small_iotas()
    stage_halos(place, (rx1, rx2), (ry1, ry2), xh, yh, 3)
    zh[...] = rz[...].astype(F32)

    def step(x, x_below, x_above):
        sides = columns(place, zh[...], x)
        for r in range(4):
            weights = stored_weights(x, r, wx, wyl, wyh, wzl, wzh)
            cells = [
                [load(ref, x, half, r) for ref in (coup, gain, keep, push)] for half in range(2)
            ]
            found = sum_sides(
                place, sub, lane, x, r, u, yh, sides, x_below, x_above, weights
            )
            update(traction, found, cells, x, r, new, strips)

    over_planes(
        step,
        lambda side, c, half, r: halo_plane(xh, side, c, half, r),
        lambda x, c, half, r: load(u, x, half, r, c),
    )
    emit_faces(place, [(new, (c,)) for c in range(3)], strips, (xs1, xs2), (ys1, ys2))
    zs[...] = ZFace(place).whole(new).astype(BF16)


def energy_kernel(
    u, tanh, wx, wyl, wyh, wzl, wzh, coup, diag, extension, rx1, rx2, ry1, ry2, rz, held,
    out, xh, yh, zh,
):
    place = Place()
    sub, lane = small_iotas()
    stage_halos(place, (rx1, rx2), (ry1, ry2), xh, yh, 3)
    zh[...] = rz[...].astype(F32)

    def step(x, x_below, x_above):
        sides = columns(place, zh[...], x)
        values = [[], []]
        for r in range(4):
            weights = stored_weights(x, r, wx, wyl, wyh, wzl, wzh)
            found = sum_sides(
                place, sub, lane, x, r, u, yh, sides, x_below, x_above, weights
            )
            for half in range(2):
                shared = found[0][0][half] + found[1][0][half] + found[2][0][half]
                shared = load(coup, x, half, r) * shared
                total = load(diag, x, half, r)
                energy = None
                for c in range(3):
                    tile, near = found[c][0][half], found[c][1][half]
                    term = tile * (total * tile + shared - near)
                    energy = term if energy is None else energy + term
                bent = load(tanh, x, half, r)
                values[half].append((0.5 - 0.5 * bent * bent) * energy)
        for half in range(2):
            whole = jnp.concatenate(values[half], axis=0)
            out[x + x // 4, :, HALVES[half]] = whole.astype(BF16)

    over_planes(
        step,
        lambda side, c, half, r: halo_plane(xh, side, c, half, r),
        lambda x, c, half, r: load(u, x, half, r, c),
    )
    for part in range(8):
        out[5 * part + 4] = extension[...]


def unpack_kernel(u, out, token, natural, sems):
    copies = []
    token[...] = jnp.zeros_like(token)
    for c in range(3):

        def step(block, carry):
            for k in range(2):
                x = block * 2 + k
                for half, r in CELLS:
                    store_natural(natural, x, half, r, load(u, x, half, r, c), c)
            return carry

        lax.fori_loop(0, CX // 2, step, 0)
        for h, half in enumerate(HALVES):
            one = pltpu.make_async_copy(natural.at[c, h], out.at[c, :, :, half], sems.at[c, h])
            one.start()
            copies.append(one)
    for one in copies:
        one.wait()


def product_kernel(received, out):
    matrix = jnp.concatenate([received[5 * part + 4] for part in range(8)], axis=0)
    for x in range(4):
        field = jnp.concatenate([received[5 * part + x] for part in range(8)], axis=0)
        moved = jnp.dot(matrix, field, preferred_element_type=F32).astype(BF16)
        for part in range(8):
            out[4 * part + x] = moved[CY * part : CY * (part + 1)]


def slopes_kernel(lev, rx1, rx2, ry1, ry2, rz, grow, shrink, xh, yh, zh):
    place = Place()
    sub, lane = small_iotas()
    near, far = rx1[3].astype(F32), rx2[3].astype(F32)
    xh[0] = jnp.where(place.even_x, far, near) * place.x_lo
    xh[1] = jnp.where(place.even_x, near, far) * place.x_hi
    near, far = ry1[3].astype(F32), ry2[3].astype(F32)
    low = jnp.where(place.even_y, far, near) * place.y_lo
    high = jnp.where(place.even_y, near, far) * place.y_hi
    for h, half in enumerate(HALVES):
        yh[0, h] = low[:, half]
        yh[1, h] = high[:, half]
    zh[0] = rz[...].astype(F32) * place.z_lo
    zh[1] = rz[...].astype(F32) * place.z_hi

    def root(total):
        return total * lax.rsqrt(jnp.maximum(total, TINY))

    def step(x, x_below, x_above):
        low_side, high_side = column(place, zh[0], 96 + x), column(place, zh[1], 96 + x)
        for r in range(4):
            part = slice(r * 8, r * 8 + 8)
            centre = [load(lev, x, half, r) for half in range(2)]
            z_below, z_above = z_sides(lane, centre, low_side[part], high_side[part])
            for half in range(2):
                mid = centre[half]
                y_pair = y_sides(
                    sub,
                    r,
                    lambda row: load(lev, x, half, row),
                    lambda: yh[0, half, pl.ds(x, 8, stride=0), :],
                    lambda: yh[1, half, pl.ds(x, 8, stride=0), :],
                )
                growing, shrinking = 0.0, 0.0
                x_pair = (x_below(half, r), x_above(half, r))
                for below, above in (x_pair, y_pair, (z_below[half], z_above[half])):
                    up = jnp.maximum(mid - jnp.minimum(below, above), 0.0)
                    down = jnp.maximum(jnp.maximum(below, above) - mid, 0.0)
                    growing = growing + up * up
                    shrinking = shrinking + down * down
                store(grow, x, half, r, ADVANCE * root(growing))
                store(shrink, x, half, r, ADVANCE * root(shrinking))

    over_planes(
        step,
        lambda side, half, r: xh[side, r * 8 : r * 8 + 8, HALVES[half]],
        lambda x, half, r: load(lev, x, half, r),
    )


def final_kernel(
    counts, listing, lev, velocity, grow, shrink, out, first, second, sign, ways, natural, sems
):
    gx, gy, ga = lax.axis_index("gx"), lax.axis_index("gy"), lax.axis_index("ga")
    sub, lane = small_iotas()
    own = counts[gx, gy * lax.axis_size("ga") + ga]
    listed = []
    for half in range(2):
        tile = lane // TILE + half * (LANES // TILE)
        mask = jnp.zeros((8, LANES), F32)
        for entry in range(CZ // TILE):
            hit = jnp.where(entry < own, listing[0, entry], -1)
            mask = jnp.where(tile == hit, PSEUDO, mask)
        listed.append(mask)
    low_z, high_z = lane % TILE == 0, lane % TILE == TILE - 1

    def advance(block, carry):
        for k in range(4):
            x = block * 4 + k
            for half in range(2):
                plane = velocity[x, :, HALVES[half]].astype(F32)
                for r in range(4):
                    moved = plane[r * 8 : r * 8 + 8]
                    speed = moved / (1.0 + jnp.abs(moved))
                    ahead = jnp.where(moved > 0.0, load(grow, x, half, r), load(shrink, x, half, r))
                    value = load(lev, x, half, r) - speed * ahead
                    store(first, x, half, r, value)
                    store(sign, x, half, r, listed[half] * (value * lax.rsqrt(value * value + 1.0)))
                    store(ways, x, half, r, jnp.where(value > 0.0, 1.0, -1.0))
        return carry

    lax.fori_loop(0, CX // 4, advance, 0)

    def sweep(source, x, half, r):
        centre = load(source, x, half, r)
        strength = load(sign, x, half, r)
        way = load(ways, x, half, r)
        sides = (
            (
                load(source, jnp.maximum(x - 1, 0), half, r),
                load(source, jnp.minimum(x + 1, CX - 1), half, r),
            ),
            y_sides(
                sub, r, lambda row: load(source, x, half, row), lambda: centre, lambda: centre
            ),
            (
                jnp.where(low_z, centre, pltpu.roll(centre, 1, 1)),
                jnp.where(high_z, centre, pltpu.roll(centre, LANES - 1, 1)),
            ),
        )
        faced = way * centre
        total = None
        for below, above in sides:
            rise = jnp.maximum(faced - jnp.minimum(way * below, way * above), 0.0)
            total = rise * rise if total is None else total + rise * rise
        root = total * lax.rsqrt(jnp.maximum(total, TINY))
        return centre - strength * (root - 1.0)

    buffers = [first, second]
    for turn in range(SWEEPS - 1):
        source, target = buffers[turn % 2], buffers[(turn + 1) % 2]

        def step(block, carry):
            for k in range(4):
                x = block * 4 + k
                for half, r in CELLS:
                    store(target, x, half, r, sweep(source, x, half, r))
            return carry

        lax.fori_loop(0, CX // 4, step, 0)
    source = buffers[(SWEEPS - 1) % 2]
    copies = []
    for i in range(CX // CHUNK):

        def last(block, carry):
            for k in range(4):
                x = i * CHUNK + block * 4 + k
                for half, r in CELLS:
                    store_natural(natural, x, half, r, sweep(source, x, half, r))
            return carry

        lax.fori_loop(0, CHUNK // 4, last, 0)
        part = pl.ds(i * CHUNK, CHUNK)
        for h, half in enumerate(HALVES):
            one = pltpu.make_async_copy(natural.at[h, part], out.at[part, :, half], sems.at[i, h])
            one.start()
            copies.append(one)
    for one in copies:
        one.wait()


def exchange(xs1, xs2, ys1, ys2, zs):
    return (
        lax.ppermute(xs1, "gx", SWAP_NEAR),
        lax.ppermute(xs2, "gx", SWAP_FAR),
        lax.ppermute(ys1, "gy", SWAP_NEAR),
        lax.ppermute(ys2, "gy", SWAP_FAR),
        lax.ppermute(zs, "ga", SWAP_Z),
    )


def faces(count):
    return [shape(count, 32, CZ, dtype=BF16)] * 4 + [shape(CY, LANES, dtype=BF16)]


def halo_scratch(count):
    return [pltpu.VMEM((2, count, CY, CZ), F32), pltpu.VMEM((2, count, 2, CX, LANES), F32)]


def local(
    level_set, displacement_prev, traction, load_mask, support_mask, extension, tile_count, tile_list
):
    displacement_prev, level_set, support_mask, load_mask = (
        pltpu.with_memory_space_constraint(x, pltpu.HBM)
        for x in (displacement_prev, level_set, support_mask, load_mask)
    )
    flat = shape(2, ROWS, LANES)
    field = shape(3, 2, ROWS, LANES)
    column_scratch = pltpu.VMEM((CY, LANES), F32)
    u, lev, free, *sent = call(
        pack_kernel,
        [field, flat, flat] + faces(4),
        [
            pltpu.VMEM((3, 2, CX, CY, LANES), F32),
            pltpu.VMEM((2, CX, CY, LANES), F32),
            pltpu.VMEM((2, CX, CY, LANES), jnp.int32),
            pltpu.SemaphoreType.DMA((CX // CHUNK, 10)),
        ]
        + strip_scratch(4),
        (displacement_prev, level_set, support_mask),
        [ANY] * 3,
    )
    got = exchange(*sent)
    level_got = got
    tanh, loaded, turned = call(
        prepare_kernel,
        [flat] * 2 + [shape(CY, NY, dtype=BF16)],
        [pltpu.VMEM((2, CX, CY, LANES), jnp.int32), pltpu.SemaphoreType.DMA((2,))],
        (lev, load_mask, extension),
        [VM, ANY, VM],
    )
    u, *rest = call(
        first_kernel,
        [field] + faces(3) + [shape(2, ROWS + CY, LANES)] + [flat] * 9,
        halo_scratch(4) + [pltpu.VMEM((3, CY, LANES), F32)] + strip_scratch(3),
        (traction, u, lev, free, tanh, loaded, *got),
        [SM] + [VM] * 10,
    )
    sent, made = rest[:5], rest[5:]
    got = exchange(*sent)
    grow, shrink = call(
        slopes_kernel, [flat] * 2,
        [pltpu.VMEM((2, CY, CZ), F32), pltpu.VMEM((2, 2, CX, LANES), F32)]
        + [pltpu.VMEM((2, CY, LANES), F32)],
        (lev, *level_got),
    )
    for turn in range(2):
        u, *sent = call(
            sweep_kernel, [field] + faces(3),
            halo_scratch(3) + [column_scratch] + strip_scratch(3),
            (traction, u, *made, *got, grow),
            [SM] + [VM] * (len(made) + 6) + [LOOSE],
        )
        got = exchange(*sent)
    displacement, token = call(
        unpack_kernel, [shape(3, CX, CY, CZ), shape(8, LANES)],
        [pltpu.VMEM((3, 2, CX, CY, LANES), F32), pltpu.SemaphoreType.DMA((3, 2))],
        (u,), None, [ANY, VM],
    )
    (sensitivity,) = call(
        energy_kernel, [shape(40, CY, CZ, dtype=BF16)], halo_scratch(3) + [column_scratch],
        (u, tanh, *made[:7], turned, *got, token),
    )
    sensitivity = lax.all_to_all(sensitivity, "gy", split_axis=0, concat_axis=0, tiled=True)
    (velocity,) = call(product_kernel, [shape(CX, CY, CZ, dtype=BF16)], [], (sensitivity,))
    velocity = lax.all_to_all(velocity, "gy", split_axis=0, concat_axis=0, tiled=True)
    (level_new,) = call(
        final_kernel, [shape(CX, CY, CZ)],
        [pltpu.VMEM((2, ROWS, LANES), F32)] * 4
        + [pltpu.VMEM((2, CX, CY, LANES), F32), pltpu.SemaphoreType.DMA((CX // CHUNK, 2))],
        (tile_count, tile_list, lev, velocity, grow, shrink),
        [SM, SM] + [VM] * 4,
        [ANY],
    )
    return (displacement, level_new)


def solution(mesh):
    return jax.shard_map(
        local,
        mesh=mesh,
        in_specs=(
            P("gx", "gy", "ga"),
            P(None, "gx", "gy", "ga"),
            P(),
            P("gx", "gy", "ga"),
            P("gx", "gy", "ga"),
            P("gy", None),
            P(),
            P(("gx", "gy", "ga"), None),
        ),
        out_specs=(P(None, "gx", "gy", "ga"), P("gx", "gy", "ga")),
        check_vma=False,
    )
```
